512 devices in a mesh: panel: 8 (over x, core), leaf: 64 (over y, z).
Axes of the slice: x: 4, y: 4, z: 16, core: 2. Of those that a mesh axis runs over, the one named last changes fastest.
Arguments:
- sources: bfloat16 [8, 3328, 2, 1536], P('panel', 'leaf'), may hold values from -6 to 6
- transmission: float32 [8, 3328, 128], P('panel', 'leaf')
- media: int32 [8, 3328, 1], P('panel', 'leaf'), may hold values from 0 to 63; in each aligned block of 52 rows (0 to 51, 52 to 103, ..., all dimensions but the last counted through in order) at most 2 rows name the same one
- sep_code: int32 [8, 64], P('panel', 'leaf'), may hold values from 0 to 7
- leaf_factors: bfloat16 [64, 2, 768, 768], P('leaf'), may hold values from -0.15625 to 0.15625
- sep_factors: bfloat16 [2, 2, 384, 384], replicated, may hold values from -0.15625 to 0.15625
Outputs:
- solutions: bfloat16 [8, 3328, 2, 1536], P('panel', 'leaf')
The draws below stay inside these ranges and needn't reach their ends.
Inputs may be any that keep to these rules, and one draw needn't show every extreme that they name: `media`: among the 52 leaves of one device (aligned blocks of rows) no library entry is named more than 2 times, a bound that some block reaches.
All inputs are finite; a program needn't handle non-finite values.
Results may differ from the reference program's by a relative error of at most 0.0065.
Values may be sent and summed in bfloat16 or wider, within the bound.
A program may use at most 64 MiB of HBM per device.

```python
import math
import jax
import jax.numpy as jnp
import numpy as np
from jax import lax

LEAF_N = 768
SEP_N = 384
FRONT = 64
SEP_LIB = 2
SHOTS = 2
LEAVES_DEV = 52
LIB = 64
LEAVES = 3328
CAP = 2
N_PANEL = 8
N_LEAF = 64


def draw_transmission(key, part):
    random_keys = jax.random.split(key, 5)
    shape_leaf = (1, LEAVES, FRONT)
    full_extent = (N_PANEL, LEAVES, FRONT)
    low_log = math.log(0.05 / N_PANEL)
    high_log = math.log(3.0)
    decay_rate = jnp.exp(jax.random.uniform(random_keys[0], shape_leaf, jnp.float32, low_log, high_log))
    panel_operator = jax.random.uniform(random_keys[1], full_extent, jnp.float32, 0.5, 2.0)
    impulse_train = jax.random.bernoulli(random_keys[2], 0.1, full_extent).astype(jnp.float32)
    impulse_penalty = jax.random.uniform(random_keys[3], full_extent, jnp.float32, 0.5, 0.8)
    field_amplitude = jnp.exp(-decay_rate * panel_operator) * (1.0 - impulse_train + impulse_train * impulse_penalty)
    phase = jax.random.uniform(random_keys[4], full_extent, jnp.float32, -math.pi, math.pi)
    return jnp.concatenate([field_amplitude * jnp.cos(phase), field_amplitude * jnp.sin(phase)], axis=-1)


def touch_ends(result, key, least, largest):
    longest = result.shape.index(max(result.shape))
    spots = []
    for shift in (0, 1):
        where = [jax.random.randint(jax.random.fold_in(key, axis), (), 0, length) for axis, length in enumerate(result.shape)]
        where[longest] = (where[longest] + shift) % result.shape[longest]
        spots.append(tuple(where))
    return result.at[spots[0]].set(least).at[spots[1]].set(largest)


def level_of(key, dims, cuts, low, high):
    loudness = 1.0
    for axis_at, blocks in cuts:
        draws = jax.random.uniform(jax.random.fold_in(jax.random.fold_in(key, 6), axis_at), (blocks,), jnp.float32, low / len(cuts), high / len(cuts))
        loudness = loudness * jnp.repeat(jnp.exp(draws), dims[axis_at] // blocks).reshape((-1,) + (1,) * (len(dims) - 1 - axis_at))
    return loudness


def deal_out(stream_key, own, number, rows, amount, top, reach, lean):
    sequence = jax.random.permutation(stream_key, amount)
    packed, usual = shares(amount, rows * top, reach, lean, True), shares(amount, rows * top, reach, lean, False)
    places = jnp.arange(amount)

    def named(tallies, turn):
        used = int((tallies > 0).sum())
        fixed = max(1, used // 4)
        moved = fixed + (places - fixed + turn * (used - fixed)) % max(1, amount - fixed)
        return jnp.zeros((amount,), jnp.int32).at[sequence[jnp.where(places < fixed, places, moved)]].set(jnp.asarray(tallies, jnp.int32))

    tallies = jnp.where(number % 4 == 0, named(packed, number // 4), named(usual, number - number // 4 - 1))
    mixed = jax.random.permutation(jax.random.fold_in(own, 3), amount)
    donor, sink = mixed[0:amount // 2 * 2:2], mixed[1:amount // 2 * 2:2]
    slack = jnp.minimum(tallies[donor] - 1, reach - tallies[sink]) // 2
    slack = jnp.where((donor == sequence[0]) | (sink == sequence[0]) | (tallies[sink] == 0), 0, jnp.maximum(slack, 0))
    moved = jax.random.randint(jax.random.fold_in(own, 4), (amount // 2,), 0, 1 << 20) % (slack + 1)
    tallies = tallies.at[donor].add(-moved).at[sink].add(moved)
    members = jnp.searchsorted(jnp.cumsum(tallies), jnp.arange(rows * top), side="right").astype(jnp.int32)
    grid = members.reshape(top, rows).T
    grid = grid[jax.random.permutation(jax.random.fold_in(own, 1), rows)]
    turn = jax.random.randint(jax.random.fold_in(own, 2), (rows, 1), 0, top)
    return jnp.take_along_axis(grid, (jnp.arange(top)[None, :] + turn) % top, axis=1)


def shares(count, total, bound, lean, full):
    weights = [(1 << 20) // math.isqrt(standing ** lean) + 1 for standing in range(1, count + 1)]
    largest = bound if full else min(bound, max(-(-total // count), total * weights[0] // sum(weights)))
    least = 1 if total - largest >= count - 1 else 0
    counts, spare = [largest] + [least] * (count - 1), total - largest - least * (count - 1)
    while spare > 0:
        movable = [i for i in range(1, count) if counts[i] < largest] or [i for i in range(1, count) if counts[i] < bound]
        pool, budget = sum([weights[i] for i in movable]), spare
        for i in movable:
            addition = min(bound - counts[i], max(1, budget * weights[i] // pool), spare)
            counts[i] = counts[i] + addition
            spare = spare - addition
    return np.array(counts)


def gaussian(own_key, dims, deviation, reach, shards=(), held_as=jnp.bfloat16):
    loudness = level_of(own_key, dims, shards, -0.22, 0.18) if shards else 1.0
    array = jax.random.normal(own_key, dims, jnp.float32) * deviation * loudness
    return jnp.minimum(jnp.maximum(array, -reach), reach).astype(held_as)


def setup_inputs(seed: int = 0) -> dict:
    streams_of = jax.random.split(jax.random.key(seed), 7)
    sources = gaussian(streams_of[0], (N_PANEL, LEAVES, SHOTS, 2 * LEAF_N), 1.0, 6.0, ((0, 8), (1, 64)))
    transmission = draw_transmission(jax.random.fold_in(streams_of[6], 71), 0)
    media_keys = jax.random.split(jax.random.fold_in(streams_of[2], 1), N_PANEL * LEAVES // LEAVES_DEV)
    media_turns = jax.random.permutation(jax.random.fold_in(streams_of[2], 3), N_PANEL * LEAVES // LEAVES_DEV)
    media = jax.vmap(lambda own, number: deal_out(jax.random.fold_in(streams_of[2], 2), own, number, LEAVES_DEV, LIB, 1, CAP, 1))(media_keys, media_turns).reshape((N_PANEL, LEAVES, 1))
    sep_code = touch_ends(jax.random.randint(streams_of[3], (N_PANEL, N_LEAF), 0, 8), jax.random.fold_in(streams_of[3], 1), 0, 7).astype(jnp.int32)
    leaf_factors = gaussian(streams_of[4], (LIB, 2, LEAF_N, LEAF_N), (2 * LEAF_N) ** -0.5, 0.15625, ((0, 64),))
    sep_factors = gaussian(streams_of[5], (SEP_LIB, 2, SEP_N, SEP_N), (4 * SEP_N) ** -0.5, 0.15625)
    return dict(sources=sources, transmission=transmission, media=media, sep_code=sep_code, leaf_factors=leaf_factors, sep_factors=sep_factors)


def complex_times(left, right, half):
    left_re, left_im = (left[..., :half], left[..., half:])
    right_re, right_im = (right[..., :half], right[..., half:])
    return jnp.concatenate([left_re * right_re - left_im * right_im, left_re * right_im + left_im * right_re], axis=-1)

def block_matrix(pair):
    real_part, imag_part = (pair[0], pair[1])
    upper = jnp.concatenate([real_part, imag_part], axis=1)
    lower = jnp.concatenate([-imag_part, real_part], axis=1)
    return jnp.concatenate([upper, lower], axis=0)

def face_rows(source, width, front):
    return jnp.concatenate([source[..., width - front:width], source[..., 2 * width - front:]], axis=-1)

def lift_face(incoming, width, front):
    gap = jnp.zeros(incoming.shape[:-1] + (width - front,), jnp.float32)
    return jnp.concatenate([gap, incoming[..., :front], gap, incoming[..., front:]], axis=-1)

def lift_top(values, width, sep):
    gap = jnp.zeros(values.shape[:-1] + (width - sep,), jnp.float32)
    return jnp.concatenate([values[..., :sep], gap, values[..., sep:], gap], axis=-1)

def trace_rows(solved, width, sep):
    return jnp.concatenate([solved[..., :sep], solved[..., width:width + sep]], axis=-1)

def reference(sources, transmission, media, sep_code, leaf_factors, sep_factors):
    face = face_rows(sources, LEAF_N, FRONT).astype(jnp.float32)

    def sweep_step(incoming, pieces):
        tau, front_src = pieces
        return (complex_times(tau[:, None, :], incoming + front_src, FRONT), incoming)
    start = jnp.zeros((LEAVES, SHOTS, 2 * FRONT), jnp.float32)
    _, arriving = lax.scan(sweep_step, start, (transmission, face))
    leaf_big = jax.vmap(block_matrix)(leaf_factors)
    sep_big = jax.vmap(block_matrix)(sep_factors)
    levels = N_LEAF.bit_length() - 1

    def one_panel(pieces):
        source, incoming, kinds, codes = pieces
        rhs = (source.astype(jnp.float32) + lift_face(incoming, LEAF_N, FRONT)).astype(jnp.bfloat16)

        def one_leaf(item):
            rows, kind = item
            return jnp.dot(rows, leaf_big[kind], preferred_element_type=jnp.float32).astype(jnp.bfloat16)
        solved = lax.map(one_leaf, (rhs, kinds[:, 0]))
        traces = trace_rows(solved.astype(jnp.float32), LEAF_N, SEP_N)
        traces = traces.reshape(N_LEAF, LEAVES_DEV, SHOTS, 2 * SEP_N).sum(axis=1)
        sep_sol = jnp.zeros((1, SHOTS, 2 * SEP_N), jnp.float32)
        for level in reversed(range(levels)):
            span = 2 ** (level + 1)
            nodes = N_LEAF // span
            block_sum = traces.reshape(nodes, span, SHOTS, 2 * SEP_N).sum(axis=1) * (1.0 / math.sqrt(LEAVES_DEV * span))
            block_code = codes.reshape(nodes, span).sum(axis=1) % SEP_LIB
            parent = jnp.repeat(sep_sol, nodes // sep_sol.shape[0], axis=0)
            operand = (block_sum - parent).astype(jnp.bfloat16)
            sep_sol = jnp.einsum('nsc,ncd->nsd', operand.astype(jnp.float32), sep_big[block_code].astype(jnp.float32))
        per_position = jnp.repeat(sep_sol, 2, axis=0)
        per_leaf = jnp.repeat(per_position, LEAVES_DEV, axis=0)
        return (solved.astype(jnp.float32) - lift_top(per_leaf, LEAF_N, SEP_N)).astype(jnp.bfloat16)
    return lax.map(one_panel, (sources, arriving, media, sep_code))
```

```python
import functools
import math

import jax
import jax.numpy as jnp
from jax import lax
from jax.experimental import pallas as pl
from jax.experimental.pallas import tpu as pltpu
from jax.sharding import PartitionSpec as P

NY = 4
ROWS = 128
MESH = pl.DeviceIdType.MESH
F32 = jnp.float32
BF16 = jnp.bfloat16


def dot(a, b):
    return jnp.dot(a, b, preferred_element_type=F32)


def kernel(
    sizes,
    src_hbm, ft_ref, trow_ref, tcol_ref, code_ref, fac_hbm, sep_hbm,
    out_ref,
    src, fac, sep, send1, sendf, recv1, recvf, face_in, acc, back1, back2, ret1, ret2, vsend, vrecv,
    load_sem, face_ss, face_rs, a2a_ss, a2a_rs, tree_ss, tree_rs,
):
    npanel, nleaf, levels, leaves = sizes
    nz = nleaf // NY
    me_p = lax.axis_index("panel")
    me = lax.axis_index("leaf")
    my_y, my_z = me // nz, me % nz

    def peer(k, sign):
        y = (my_y + sign * (k // nz) + NY) % NY
        z = (my_z + sign * (k % nz) + nz) % nz
        return {"panel": me_p, "leaf": y * nz + z}

    def panel_peer(j):
        return {"panel": (me_p + j) % npanel, "leaf": me}

    loads = [
        pltpu.make_async_copy(src_hbm, src, load_sem.at[0]),
        pltpu.make_async_copy(fac_hbm, fac, load_sem.at[1]),
        pltpu.make_async_copy(sep_hbm, sep, load_sem.at[2]),
    ]
    for load in loads:
        load.start()

    barrier = pltpu.get_barrier_semaphore()

    @pl.loop(1, nleaf)
    def _(k):
        pl.semaphore_signal(barrier, inc=1, device_id=peer(k, 1), device_id_type=MESH)

    for j in range(1, npanel):
        pl.semaphore_signal(barrier, inc=1, device_id=panel_peer(j), device_id_type=MESH)

    loads[0].wait()
    place = lax.broadcasted_iota(jnp.int32, (nleaf * 8, ROWS), 0)
    pick_re = (place == trow_ref[...]).astype(F32).astype(BF16)
    pick_im = (place == trow_ref[...] + 4).astype(F32).astype(BF16)
    packed = dot(pick_re, src[0, :, 0:640]) + dot(pick_im, src[1, :, 0:640])
    send1[...] = packed.reshape(nleaf, 8, 640).astype(BF16)
    recv1[0] = send1[0]

    pl.semaphore_wait(barrier, nleaf - 1 + npanel - 1)

    def face_copy(j):
        return pltpu.make_async_remote_copy(
            src_ref=ft_ref, dst_ref=face_in.at[j], send_sem=face_ss.at[j], recv_sem=face_rs.at[j],
            device_id=panel_peer(j), device_id_type=MESH,
        )

    for j in range(1, npanel):
        face_copy(j).start()

    def exchange(source, target, index, sign, first=1, last=None):
        @pl.loop(first, nleaf if last is None else last)
        def _(k):
            pltpu.make_async_remote_copy(
                src_ref=source.at[k], dst_ref=target.at[k], send_sem=a2a_ss.at[index],
                recv_sem=a2a_rs.at[index], device_id=peer(k, sign), device_id_type=MESH,
            ).start()

    def sent(buffer, index):
        part = buffer.at[pl.ds(1, nleaf - 1)]
        pltpu.make_async_copy(part, part, a2a_ss.at[index]).wait()

    def landed(buffer, index):
        part = buffer.at[pl.ds(1, nleaf - 1)]
        pltpu.make_async_copy(part, part, a2a_rs.at[index]).wait()

    exchange(send1, recv1, 0, 1)

    for j in range(1, npanel):
        face_copy(j).wait_recv()
    lane = lax.broadcasted_iota(jnp.int32, (ROWS, 128), 1)
    low = lane < 64

    def advance(q, arriving):
        slot = (me_p - q + npanel) % npanel
        tau = face_in[slot, 0]
        swapped = pltpu.roll(tau, 64, 1)
        tau_re = jnp.where(low, tau, swapped)
        tau_im = jnp.where(low, -swapped, tau)
        value = arriving + face_in[slot, 1]
        leaving = tau_re * value + tau_im * pltpu.roll(value, 64, 1)
        return jnp.where(q < me_p, leaving, arriving)

    arriving = jnp.zeros((ROWS, 128), F32)
    for q in range(npanel - 1):
        arriving = advance(q, arriving)
    zero = jnp.zeros((ROWS, 128), F32)
    tail_re = src[0, :, 640:768].astype(F32) + jnp.where(low, zero, pltpu.roll(arriving, 64, 1))
    tail_im = src[1, :, 640:768].astype(F32) + jnp.where(low, zero, arriving)
    packed = dot(pick_re, tail_re.astype(BF16)) + dot(pick_im, tail_im.astype(BF16))
    sendf[...] = packed.reshape(nleaf, 8, 128).astype(BF16)
    recvf[0] = sendf[0]
    exchange(sendf, recvf, 1, 1)

    loads[1].wait()
    loads[2].wait()
    landed(recv1, 0)
    rows = recv1[...].astype(F32).reshape(nleaf * 8, 640).astype(BF16)
    acc[0] = dot(rows, fac[0, 0:640, :])
    acc[1] = dot(rows, fac[1, 0:640, :])
    landed(recvf, 1)
    rows = recvf[...].astype(F32).reshape(nleaf * 8, 128).astype(BF16)
    turn = lax.broadcasted_iota(jnp.int32, (1, 8, 128), 1) < 4

    def combine(real, imag):
        width = real.shape[-1]
        real = real.reshape(-1, 8, width)
        imag = pltpu.roll(imag.reshape(-1, 8, width), 4, 1)
        sign = jnp.where(lax.broadcasted_iota(jnp.int32, imag.shape, 1) < 4, -1.0, 1.0)
        return real + sign * imag

    for half, back in ((0, back1), (1, back2)):
        cols = slice(half * 384, half * 384 + 384)
        real = acc[0, :, cols] + dot(rows, fac[0, 640:768, cols])
        imag = acc[1, :, cols] + dot(rows, fac[1, 640:768, cols])
        back[...] = combine(real, imag).astype(BF16)
        if half == 0:
            ret1[0] = back1[0]
            exchange(back1, ret1, 2, -1)
    ret2[0] = back2[0]
    cuts = [1 + (nleaf - 1) * i // 3 for i in range(4)]
    exchange(back2, ret2, 3, -1, cuts[0], cuts[1])

    landed(ret1, 2)
    total = jnp.sum(ret1[...].astype(F32), axis=0)
    eight = lax.broadcasted_iota(jnp.int32, (8, 384), 0)
    total = total + jnp.where(eight % 4 < 2, pltpu.roll(total, 6, 0), pltpu.roll(total, 2, 0))
    trace, code = total, code_ref[...]
    sums = []
    for step in range(levels // 2):
        vsend[step, :, 0:384] = trace
        vsend[step, :, 384:512] = code
        copies = []
        for j in range(1, 4):
            digit = me // 4**step % 4
            moved = (digit + 1 - 2 * (digit % 2), digit + 2 - 4 * (digit // 2), 3 - digit)[j - 1]
            other = me + (moved - digit) * 4**step
            copies.append(pltpu.make_async_remote_copy(
                src_ref=vsend.at[step], dst_ref=vrecv.at[step, j], send_sem=tree_ss.at[step, j],
                recv_sem=tree_rs.at[step, j], device_id={"panel": me_p, "leaf": other},
                device_id_type=MESH,
            ))
        for copy in copies:
            copy.start()
        if step < 2:
            exchange(back2, ret2, 3, -1, cuts[step + 1], cuts[step + 2])
        for copy in copies:
            copy.wait()
        pair_t = trace + vrecv[step, 1, :, 0:384]
        pair_c = code + vrecv[step, 1, :, 384:512]
        trace = pair_t + (vrecv[step, 2, :, 0:384] + vrecv[step, 3, :, 0:384])
        code = pair_c + (vrecv[step, 2, :, 384:512] + vrecv[step, 3, :, 384:512])
        sums += [(pair_t, pair_c), (trace, code)]

    sign8 = jnp.where(eight < 4, -1.0, 1.0)
    value = jnp.zeros((8, 384), F32)
    for level in reversed(range(levels)):
        level_sum, level_code = sums[level]
        odd = level_code - 2.0 * jnp.floor(level_code * 0.5)
        odd = jnp.concatenate([odd, odd, odd], axis=1) > 0.5
        scale = 1.0 / math.sqrt(leaves * 2 ** (level + 1))
        operand = (level_sum * scale - value).astype(BF16)
        real = jnp.where(odd, dot(operand, sep[1, 0]), dot(operand, sep[0, 0]))
        imag = jnp.where(odd, dot(operand, sep[1, 1]), dot(operand, sep[0, 1]))
        value = real + sign8 * pltpu.roll(imag, 4, 0)

    spot = lax.broadcasted_iota(jnp.int32, (ROWS, nleaf * 8), 1)
    even = lax.broadcasted_iota(jnp.int32, (ROWS, 384), 0) % 2 == 0
    take = [(spot == tcol_ref[...] + 4 * part).astype(F32).astype(BF16) for part in range(2)]
    rows = ret1[...].astype(F32).reshape(nleaf * 8, 384).astype(BF16)
    for part in range(2):
        shift = jnp.where(even, value[4 * part : 4 * part + 1], value[4 * part + 1 : 4 * part + 2])
        out_ref[:, 768 * part : 768 * part + 384] = (dot(take[part], rows) - shift).astype(BF16)
    landed(ret2, 3)
    rows = ret2[...].astype(F32).reshape(nleaf * 8, 384).astype(BF16)
    for part in range(2):
        out_ref[:, 768 * part + 384 : 768 * part + 768] = dot(take[part], rows).astype(BF16)

    for buffer, index in ((send1, 0), (sendf, 1), (back1, 2), (back2, 3)):
        sent(buffer, index)
    for j in range(1, npanel):
        face_copy(j).wait_send()


def on_device(sources, transmission, media, sep_code, leaf_factors, sep_factors):
    leaves, shots, width2 = sources.shape[1:]
    npanel, nleaf = lax.axis_size("panel"), lax.axis_size("leaf")
    levels = nleaf.bit_length() - 1
    nz = nleaf // NY
    me = lax.axis_index("leaf")
    used = leaves * shots
    source = sources[0].reshape(used, 2, width2 // 2)
    source = jnp.pad(source, ((0, ROWS - used), (0, 0), (0, 0))).transpose(1, 0, 2)
    face = jnp.concatenate([source[0, :, 704:], source[1, :, 704:]], axis=1).astype(F32)
    tau = jnp.pad(jnp.repeat(transmission[0], shots, axis=0), ((0, ROWS - used), (0, 0)))
    ft = jnp.stack([tau, face])
    kinds = media[0, :, 0]
    order = jnp.arange(leaves)
    twin = (kinds[:, None] == kinds[None, :]) & (order[None, :] < order[:, None])
    rank = jnp.sum(twin.astype(jnp.int32), axis=1)
    away = (kinds // nz - me // nz) % NY * nz + (kinds % nz - me % nz) % nz
    slot = (away * 8 + rank * 2)[:, None] + jnp.arange(shots)[None, :]
    slot = jnp.pad(slot.reshape(used), (0, ROWS - used), constant_values=-64)
    code = jnp.broadcast_to(sep_code.astype(F32), (8, 128))
    half = width2 // 2
    sem = pltpu.SemaphoreType.DMA
    vmem = pl.BlockSpec(memory_space=pltpu.VMEM)
    hbm = pl.BlockSpec(memory_space=pl.ANY)
    out = pl.pallas_call(
        functools.partial(kernel, (npanel, nleaf, levels, leaves)),
        out_shape=jax.ShapeDtypeStruct((ROWS, width2), BF16),
        in_specs=[hbm, vmem, vmem, vmem, vmem, hbm, hbm],
        out_specs=vmem,
        scratch_shapes=[
            pltpu.VMEM((2, ROWS, half), BF16),
            pltpu.VMEM((2, half, half), BF16),
            pltpu.VMEM(sep_factors.shape, BF16),
            pltpu.VMEM((nleaf, 8, 640), BF16),
            pltpu.VMEM((nleaf, 8, 128), BF16),
            pltpu.VMEM((nleaf, 8, 640), BF16),
            pltpu.VMEM((nleaf, 8, 128), BF16),
            pltpu.VMEM((npanel, 2, ROWS, 128), F32),
            pltpu.VMEM((2, nleaf * 8, half), F32),
            pltpu.VMEM((nleaf, 8, 384), BF16),
            pltpu.VMEM((nleaf, 8, 384), BF16),
            pltpu.VMEM((nleaf, 8, 384), BF16),
            pltpu.VMEM((nleaf, 8, 384), BF16),
            pltpu.VMEM((levels // 2, 8, 512), F32),
            pltpu.VMEM((levels // 2, 4, 8, 512), F32),
            sem((3,)), sem((npanel,)), sem((npanel,)), sem((4,)), sem((4,)),
            sem((levels // 2, 4)), sem((levels // 2, 4)),
        ],
        compiler_params=pltpu.CompilerParams(
            collective_id=0, has_side_effects=True, vmem_limit_bytes=48 * 1024 * 1024
        ),
    )(source, ft, slot[None, :], slot[:, None], code, leaf_factors[0], sep_factors)
    return out[:used].reshape(1, leaves, shots, width2)


def solution(mesh):
    return jax.shard_map(
        on_device,
        mesh=mesh,
        in_specs=(
            P("panel", "leaf", None, None),
            P("panel", "leaf", None),
            P("panel", "leaf", None),
            P("panel", "leaf"),
            P("leaf", None, None, None),
            P(),
        ),
        out_specs=P("panel", "leaf", None, None),
        check_vma=False,
    )
```

```python
import functools
import math

import jax
import jax.numpy as jnp
from jax import lax
from jax.experimental import pallas as pl
from jax.experimental.pallas import tpu as pltpu
from jax.sharding import PartitionSpec as P

NY = 4
ROWS = 112
MESH = pl.DeviceIdType.MESH
F32 = jnp.float32
BF16 = jnp.bfloat16
I32 = jnp.int32


def dot(a, b):
    return jnp.dot(a, b, preferred_element_type=F32)


def iota(shape, axis):
    return lax.broadcasted_iota(I32, shape, axis)


def kernel(
    sizes,
    src_hbm, tau_hbm, media_hbm, code_hbm, fac_hbm, sep_hbm,
    out_ref,
    tau_ref, media_ref, code_ref, raw, src, fac, sep, send, recv, tau_out, face_out, tau_in, face_in, back1, back2, ret1, ret2,
    csend, crecv, vsend, vrecv, chosen, top,
    load_sem, tau_ss, tau_rs, face_ss, face_rs, a2a_ss, a2a_rs, code_ss, code_rs, tree_ss, tree_rs,
):
    npanel, nleaf, levels, leaves = sizes
    nz = nleaf // NY
    used = 2 * leaves
    rounds = levels // 2
    me_p = lax.axis_index("panel")
    me = lax.axis_index("leaf")
    my_y, my_z = me // nz, me % nz

    def peer(k, sign):
        y = (my_y + sign * (k // nz) + NY) % NY
        z = (my_z + sign * (k % nz) + nz) % nz
        return {"panel": me_p, "leaf": y * nz + z}

    def panel_peer(j):
        return {"panel": (me_p + j) % npanel, "leaf": me}

    barrier = pltpu.get_barrier_semaphore()

    @pl.loop(1, nleaf)
    def _(k):
        pl.semaphore_signal(barrier, inc=1, device_id=peer(k, 1), device_id_type=MESH)

    for j in range(1, npanel):
        pl.semaphore_signal(barrier, inc=1, device_id=panel_peer(j), device_id_type=MESH)

    loads = [
        pltpu.make_async_copy(src_hbm.at[0], raw, load_sem.at[0]),
        pltpu.make_async_copy(fac_hbm.at[0], fac, load_sem.at[1]),
        pltpu.make_async_copy(sep_hbm, sep, load_sem.at[2]),
        pltpu.make_async_copy(media_hbm, media_ref, load_sem.at[3]),
        pltpu.make_async_copy(tau_hbm, tau_ref, load_sem.at[4]),
        pltpu.make_async_copy(code_hbm, code_ref, load_sem.at[5]),
    ]
    for load in loads:
        load.start()

    for load in loads[3:]:
        load.wait()
    lane = iota((ROWS, leaves), 1)
    leaf = iota((ROWS, leaves), 0) // 2
    kinds = jnp.broadcast_to(media_ref[...], (ROWS, leaves)).astype(F32)
    kind = jnp.sum(jnp.where(lane == leaf, kinds, 0.0), axis=1, keepdims=True)
    rank = jnp.sum(jnp.where((kinds == kind) & (lane < leaf), 1.0, 0.0), axis=1, keepdims=True)
    kind, rank = kind.astype(I32), rank.astype(I32)
    row = iota((ROWS, 1), 0)
    away_y = (kind // nz - my_y + NY) % NY
    away_z = (kind % nz - my_z + nz) % nz
    spot = (away_y * nz + away_z) * 8 + rank * 2 + row % 2
    spot = jnp.where(row < used, spot, -64)
    diagonal = iota((ROWS, ROWS), 0) == iota((ROWS, ROWS), 1)
    spot_row = jnp.sum(jnp.where(diagonal, spot.astype(F32), 0.0), axis=0, keepdims=True).astype(I32)
    place = iota((nleaf * 8, ROWS), 0)
    pick = [(place == spot_row + 4 * part).astype(F32).astype(BF16) for part in range(2)]

    tau_out[0:leaves, :] = tau_ref[...].reshape(leaves, 128)
    tau_out[leaves:56, :] = jnp.zeros((56 - leaves, 128), F32)
    loads[0].wait()
    rows = raw[...].astype(F32).reshape(used, 1536)
    src[...] = jnp.concatenate([rows, jnp.zeros((ROWS - used, 1536), F32)], axis=0).astype(BF16)
    low = iota((ROWS, 128), 1) < 64
    tile_re, tile_im = src[:, 640:768].astype(F32), src[:, 1408:1536].astype(F32)
    face_out[...] = jnp.where(low, pltpu.roll(tile_re, 64, 1), tile_im).astype(BF16)
    packed = dot(pick[0], src[:, 0:640]) + dot(pick[1], src[:, 768:1408])
    send[:, :, 0:640] = packed.reshape(nleaf, 8, 640).astype(BF16)
    csend[0] = jnp.broadcast_to(code_ref[...].astype(F32), (8, 128))

    pl.semaphore_wait(barrier, nleaf - 1 + npanel - 1)

    def face_copies(j):
        return [
            pltpu.make_async_remote_copy(
                src_ref=tau_out, dst_ref=tau_in.at[j], send_sem=tau_ss.at[j],
                recv_sem=tau_rs.at[j], device_id=panel_peer(j), device_id_type=MESH,
            ),
            pltpu.make_async_remote_copy(
                src_ref=face_out, dst_ref=face_in.at[j], send_sem=face_ss.at[j],
                recv_sem=face_rs.at[j], device_id=panel_peer(j), device_id_type=MESH,
            ),
        ]

    for j in range(1, npanel):
        for copy in face_copies(j):
            copy.start()

    def exchange(source, target, index, sign, first, last, cols):
        @pl.loop(max(first, 1), last)
        def _(k):
            pltpu.make_async_remote_copy(
                src_ref=source.at[k, :, cols], dst_ref=target.at[k, :, cols],
                send_sem=a2a_ss.at[index], recv_sem=a2a_rs.at[index],
                device_id=peer(k, sign), device_id_type=MESH,
            ).start()

    def wait_for(sems, buffer, index, first, last, cols):
        part = buffer.at[pl.ds(max(first, 1), last - max(first, 1)), :, cols]
        pltpu.make_async_copy(part, part, sems.at[index]).wait()

    def tree_copies(step, source, target, ss, rs):
        copies = []
        for j in range(1, 4):
            digit = me // 4**step % 4
            moved = (digit + 1 - 2 * (digit % 2), digit + 2 - 4 * (digit // 2), 3 - digit)[j - 1]
            other = me + (moved - digit) * 4**step
            copies.append(pltpu.make_async_remote_copy(
                src_ref=source.at[step], dst_ref=target.at[step, j], send_sem=ss.at[step, j],
                recv_sem=rs.at[step, j], device_id={"panel": me_p, "leaf": other},
                device_id_type=MESH,
            ))
        return copies

    def two_levels(own, got, step):
        pair = own + got[step, 1]
        return pair, pair + (got[step, 2] + got[step, 3])

    bulk, tail, whole = pl.ds(0, 640), pl.ds(640, 128), pl.ds(0, 768)
    half = pl.ds(0, 384)
    cuts = [nleaf * i // 4 for i in range(5)]
    early = 2
    codes = []
    for step in range(rounds):
        copies = tree_copies(step, csend, crecv, code_ss, code_rs)
        for copy in copies:
            copy.start()
        if step < early:
            exchange(send, recv, step, 1, cuts[step], cuts[step + 1], bulk)
        for copy in copies:
            copy.wait()
        codes += two_levels(csend[step], crecv, step)
        if step + 1 < rounds:
            csend[step + 1] = codes[-1]

    for j in range(1, npanel):
        for copy in face_copies(j):
            copy.wait_recv()
    arriving = jnp.zeros((ROWS, 128), F32)
    for q in range(npanel - 1):
        slot = (me_p - q + npanel) % npanel
        tau = jnp.broadcast_to(tau_in[slot].reshape(56, 1, 128), (56, 2, 128)).reshape(ROWS, 128)
        swapped = pltpu.roll(tau, 64, 1)
        tau_re = jnp.where(low, tau, swapped)
        tau_im = jnp.where(low, -swapped, tau)
        value = arriving + face_in[slot].astype(F32)
        leaving = tau_re * value + tau_im * pltpu.roll(value, 64, 1)
        arriving = jnp.where(q < me_p, leaving, arriving)
    zero = jnp.zeros((ROWS, 128), F32)
    tile_re = src[:, 640:768].astype(F32) + jnp.where(low, zero, pltpu.roll(arriving, 64, 1))
    tile_im = src[:, 1408:1536].astype(F32) + jnp.where(low, zero, arriving)
    packed = dot(pick[0], tile_re.astype(BF16)) + dot(pick[1], tile_im.astype(BF16))
    send[:, :, 640:768] = packed.reshape(nleaf, 8, 128).astype(BF16)
    recv[0] = send[0]
    for g in range(early):
        exchange(send, recv, 4 + g, 1, cuts[g], cuts[g + 1], tail)
    for g in range(early, 4):
        exchange(send, recv, g, 1, cuts[g], cuts[g + 1], whole)

    loads[1].wait()
    loads[2].wait()
    for level in range(levels):
        count = codes[level][0:1, 0:1]
        odd = (count - 2.0 * jnp.floor(count * 0.5)).astype(BF16)
        odd = jnp.broadcast_to(odd, (384, 384))
        for part in range(2):
            chosen[level, :, 384 * part : 384 * part + 384] = (
                sep[0, part] * (1 - odd) + sep[1, part] * odd
            )

    def combine(real, imag):
        real = real.reshape(-1, 8, 384)
        imag = pltpu.roll(imag.reshape(-1, 8, 384), 4, 1)
        return real + jnp.where(iota(imag.shape, 1) < 4, -1.0, 1.0) * imag

    for g in range(4):
        first, last = cuts[g], cuts[g + 1]
        wait_for(a2a_rs, recv, g, first, last, bulk if g < early else whole)
        if g < early:
            wait_for(a2a_rs, recv, 4 + g, first, last, tail)
        rows = recv[first:last].astype(F32).reshape((last - first) * 8, 768).astype(BF16)
        for part, back in ((0, back1), (1, back2)):
            cols = slice(part * 384, part * 384 + 384)
            result = combine(dot(rows, fac[0, :, cols]), dot(rows, fac[1, :, cols]))
            back[first:last] = result.astype(BF16)
            if part == 0:
                exchange(back1, ret1, 6 + g, -1, first, last, half)
    ret1[0] = back1[0]
    ret2[0] = back2[0]
    turns = [1, 12, 24, 46, nleaf]
    exchange(back2, ret2, 10, -1, turns[0], turns[1], half)

    for g in range(4):
        wait_for(a2a_rs, ret1, 6 + g, cuts[g], cuts[g + 1], half)
    total = jnp.sum(ret1[...].astype(F32), axis=0)
    eight = iota((8, 384), 0)
    total = total + jnp.where(eight % 4 < 2, pltpu.roll(total, 6, 0), pltpu.roll(total, 2, 0))
    sums = []
    spots = iota((ROWS, nleaf * 8), 1)
    take = [(spots == spot + 4 * part).astype(F32).astype(BF16) for part in range(2)]
    for step in range(rounds):
        vsend[step] = total
        copies = tree_copies(step, vsend, vrecv, tree_ss, tree_rs)
        for copy in copies:
            copy.start()
        exchange(back2, ret2, 10, -1, turns[step + 1], turns[step + 2], half)
        if step == 0:
            rows = ret1[...].astype(F32).reshape(nleaf * 8, 384).astype(BF16)
            for part in range(2):
                top[part] = dot(take[part], rows)
        for copy in copies:
            copy.wait()
        sums += two_levels(total, vrecv, step)
        total = sums[-1]

    sign8 = jnp.where(eight < 4, -1.0, 1.0)
    value = jnp.zeros((8, 384), F32)
    for level in reversed(range(levels)):
        scale = 1.0 / math.sqrt(leaves * 2 ** (level + 1))
        operand = (sums[level] * scale - value).astype(BF16)
        both = dot(operand, chosen[level])
        value = both[:, 0:384] + sign8 * pltpu.roll(both[:, 384:768], 4, 0)

    even = iota((ROWS, 384), 0) % 2 == 0
    for part in range(2):
        shift = jnp.where(even, value[4 * part : 4 * part + 1], value[4 * part + 1 : 4 * part + 2])
        out_ref[:, 768 * part : 768 * part + 384] = (top[part] - shift).astype(BF16)
    wait_for(a2a_rs, ret2, 10, 0, nleaf, half)
    rows = ret2[...].astype(F32).reshape(nleaf * 8, 384).astype(BF16)
    for part in range(2):
        out_ref[:, 768 * part + 384 : 768 * part + 768] = dot(take[part], rows).astype(BF16)

    for g in range(4):
        wait_for(a2a_ss, send, g, cuts[g], cuts[g + 1], bulk if g < early else whole)
        if g < early:
            wait_for(a2a_ss, send, 4 + g, cuts[g], cuts[g + 1], tail)
        wait_for(a2a_ss, back1, 6 + g, cuts[g], cuts[g + 1], half)
    wait_for(a2a_ss, back2, 10, 0, nleaf, half)
    for j in range(1, npanel):
        for copy in face_copies(j):
            copy.wait_send()


def on_device(sources, transmission, media, sep_code, leaf_factors, sep_factors):
    leaves, shots, width2 = sources.shape[1:]
    npanel, nleaf = lax.axis_size("panel"), lax.axis_size("leaf")
    levels = nleaf.bit_length() - 1
    rounds = levels // 2
    half = width2 // 2
    sem = pltpu.SemaphoreType.DMA
    vmem = pl.BlockSpec(memory_space=pltpu.VMEM)
    hbm = pl.BlockSpec(memory_space=pl.ANY)
    out = pl.pallas_call(
        functools.partial(kernel, (npanel, nleaf, levels, leaves)),
        out_shape=jax.ShapeDtypeStruct((ROWS, width2), BF16),
        in_specs=[hbm] * 6,
        out_specs=vmem,
        scratch_shapes=[
            pltpu.VMEM((leaves, 1, 128), F32),
            pltpu.VMEM((1, leaves), I32),
            pltpu.VMEM((1, 1), I32),
            pltpu.VMEM((leaves, shots, width2), BF16),
            pltpu.VMEM((ROWS, width2), BF16),
            pltpu.VMEM((2, half, half), BF16),
            pltpu.VMEM(sep_factors.shape, BF16),
            pltpu.VMEM((nleaf, 8, half), BF16),
            pltpu.VMEM((nleaf, 8, half), BF16),
            pltpu.VMEM((ROWS // 2, 128), F32),
            pltpu.VMEM((ROWS, 128), BF16),
            pltpu.VMEM((npanel, ROWS // 2, 128), F32),
            pltpu.VMEM((npanel, ROWS, 128), BF16),
            pltpu.VMEM((nleaf, 8, 384), BF16),
            pltpu.VMEM((nleaf, 8, 384), BF16),
            pltpu.VMEM((nleaf, 8, 384), BF16),
            pltpu.VMEM((nleaf, 8, 384), BF16),
            pltpu.VMEM((rounds, 8, 128), F32),
            pltpu.VMEM((rounds, 4, 8, 128), F32),
            pltpu.VMEM((rounds, 8, 384), F32),
            pltpu.VMEM((rounds, 4, 8, 384), F32),
            pltpu.VMEM((levels, 384, 768), BF16),
            pltpu.VMEM((2, ROWS, 384), F32),
            sem((6,)), sem((npanel,)), sem((npanel,)), sem((npanel,)), sem((npanel,)),
            sem((11,)), sem((11,)), sem((rounds, 4)), sem((rounds, 4)), sem((rounds, 4)),
            sem((rounds, 4)),
        ],
        compiler_params=pltpu.CompilerParams(
            collective_id=0, has_side_effects=True, vmem_limit_bytes=67043328
        ),
    )(
        sources, transmission.transpose(1, 0, 2), media.reshape(1, leaves), sep_code,
        leaf_factors, sep_factors,
    )
    return out[: leaves * shots].reshape(1, leaves, shots, width2)


def solution(mesh):
    return jax.shard_map(
        on_device,
        mesh=mesh,
        in_specs=(
            P("panel", "leaf", None, None),
            P("panel", "leaf", None),
            P("panel", "leaf", None),
            P("panel", "leaf"),
            P("leaf", None, None, None),
            P(),
        ),
        out_specs=P("panel", "leaf", None, None),
        check_vma=False,
    )
```

```python
import functools
import math

import jax
import jax.numpy as jnp
from jax import lax
from jax.experimental import pallas as pl
from jax.experimental.pallas import tpu as pltpu
from jax.sharding import PartitionSpec as P

NY = 4
ROWS = 112
MESH = pl.DeviceIdType.MESH
F32 = jnp.float32
BF16 = jnp.bfloat16
I32 = jnp.int32


def dot(a, b):
    return jnp.dot(a, b, preferred_element_type=F32)


def iota(shape, axis):
    return lax.broadcasted_iota(I32, shape, axis)


def kernel(
    sizes,
    src_hbm, tau_hbm, media_hbm, code_hbm, fac_hbm, sep_hbm,
    out_ref,
    tau_ref, media_ref, code_ref, raw, src, fac, sep, send, recv, tau_out, face_out, tau_in, face_in, back1, back2, ret1, ret2,
    csend, crecv, vsend, vrecv, ysend, esend, erecv, chosen, top,
    far_sem, load_sem, tau_ss, tau_rs, face_ss, face_rs, a2a_ss, a2a_rs, code_ss, code_rs, tree_ss, tree_rs,
    node_ss, node_rs,
):
    npanel, nleaf, levels, leaves = sizes
    nz = nleaf // NY
    used = 2 * leaves
    rounds = levels // 2
    me_p = lax.axis_index("panel")
    me = lax.axis_index("leaf")
    my_y, my_z = me // nz, me % nz

    def peer(k, sign):
        order = k // NY
        steps = (order % 2) * ((order + 1) // 2) - (1 - order % 2) * (order // 2)
        y = (my_y + sign * (k % NY) + NY) % NY
        z = (my_z + sign * steps + nz) % nz
        return {"panel": me_p, "leaf": y * nz + z}

    reach = nz // 4
    near = (2 * reach + 1) * NY

    def panel_peer(j):
        return {"panel": (me_p + j) % npanel, "leaf": me}

    barrier = pltpu.get_barrier_semaphore()

    @pl.loop(1, near)
    def _(k):
        pl.semaphore_signal(barrier, inc=1, device_id=peer(k, 1), device_id_type=MESH)

    for j in range(1, npanel):
        pl.semaphore_signal(barrier, inc=1, device_id=panel_peer(j), device_id_type=MESH)

    loads = [
        pltpu.make_async_copy(src_hbm.at[0], raw, load_sem.at[0]),
        pltpu.make_async_copy(fac_hbm.at[0], fac, load_sem.at[1]),
        pltpu.make_async_copy(sep_hbm, sep, load_sem.at[2]),
        pltpu.make_async_copy(media_hbm, media_ref, load_sem.at[3]),
        pltpu.make_async_copy(tau_hbm, tau_ref, load_sem.at[4]),
        pltpu.make_async_copy(code_hbm, code_ref, load_sem.at[5]),
    ]
    for load in loads:
        load.start()

    for load in loads[3:]:
        load.wait()
    lane = iota((ROWS, leaves), 1)
    leaf = iota((ROWS, leaves), 0) // 2
    kinds = jnp.broadcast_to(media_ref[...], (ROWS, leaves)).astype(F32)
    kind = jnp.sum(jnp.where(lane == leaf, kinds, 0.0), axis=1, keepdims=True)
    rank = jnp.sum(jnp.where((kinds == kind) & (lane < leaf), 1.0, 0.0), axis=1, keepdims=True)
    kind, rank = kind.astype(I32), rank.astype(I32)
    row = iota((ROWS, 1), 0)
    away_y = (kind // nz - my_y + NY) % NY
    away_z = (kind % nz - my_z + nz) % nz
    order = jnp.where(away_z <= nz // 2, 2 * away_z - 1, 2 * (nz - away_z))
    order = jnp.maximum(order, 0)
    spot = (order * NY + away_y) * 8 + rank * 2 + row % 2
    spot = jnp.where(row < used, spot, -64)
    diagonal = iota((ROWS, ROWS), 0) == iota((ROWS, ROWS), 1)
    spot_row = jnp.sum(jnp.where(diagonal, spot.astype(F32), 0.0), axis=0, keepdims=True).astype(I32)
    place = iota((nleaf * 8, ROWS), 0)
    pick = [(place == spot_row + 4 * part).astype(F32).astype(BF16) for part in range(2)]

    tau_out[0:leaves, :] = tau_ref[...].reshape(leaves, 128)
    tau_out[leaves:56, :] = jnp.zeros((56 - leaves, 128), F32)
    loads[0].wait()
    rows = raw[...].astype(F32).reshape(used, 1536)
    src[...] = jnp.concatenate([rows, jnp.zeros((ROWS - used, 1536), F32)], axis=0).astype(BF16)
    low = iota((ROWS, 128), 1) < 64
    tile_re, tile_im = src[:, 640:768].astype(F32), src[:, 1408:1536].astype(F32)
    face_out[...] = jnp.where(low, pltpu.roll(tile_re, 64, 1), tile_im).astype(BF16)
    packed = dot(pick[0], src[:, 0:640]) + dot(pick[1], src[:, 768:1408])
    send[:, :, 0:640] = packed.reshape(nleaf, 8, 640).astype(BF16)
    csend[0] = jnp.broadcast_to(code_ref[...].astype(F32), (8, 128))

    pl.semaphore_wait(barrier, near - 1 + npanel - 1)
    for order in (2 * reach - 1, 2 * reach):
        pl.semaphore_signal(far_sem, inc=1, device_id=peer(order * NY, 1), device_id_type=MESH)

    def face_copies(j):
        return [
            pltpu.make_async_remote_copy(
                src_ref=tau_out, dst_ref=tau_in.at[j], send_sem=tau_ss.at[j],
                recv_sem=tau_rs.at[j], device_id=panel_peer(j), device_id_type=MESH,
            ),
            pltpu.make_async_remote_copy(
                src_ref=face_out, dst_ref=face_in.at[j], send_sem=face_ss.at[j],
                recv_sem=face_rs.at[j], device_id=panel_peer(j), device_id_type=MESH,
            ),
        ]

    for j in range(1, npanel):
        for copy in face_copies(j):
            copy.start()

    def exchange(source, target, index, sign, first, last, cols):
        @pl.loop(max(first, 1), last)
        def _(k):
            pltpu.make_async_remote_copy(
                src_ref=source.at[k, :, cols], dst_ref=target.at[k, :, cols],
                send_sem=a2a_ss.at[index], recv_sem=a2a_rs.at[index],
                device_id=peer(k, sign), device_id_type=MESH,
            ).start()

    def wait_for(sems, buffer, index, first, last, cols):
        part = buffer.at[pl.ds(max(first, 1), last - max(first, 1)), :, cols]
        pltpu.make_async_copy(part, part, sems.at[index]).wait()

    def tree_copies(step, source, target, ss, rs):
        copies = []
        for j in range(1, 4):
            digit = me // 4**step % 4
            moved = (digit + 1 - 2 * (digit % 2), digit + 2 - 4 * (digit // 2), 3 - digit)[j - 1]
            other = me + (moved - digit) * 4**step
            copies.append(pltpu.make_async_remote_copy(
                src_ref=source.at[step], dst_ref=target.at[step, j], send_sem=ss.at[step, j],
                recv_sem=rs.at[step, j], device_id={"panel": me_p, "leaf": other},
                device_id_type=MESH,
            ))
        return copies

    def two_levels(own, got, step):
        pair = own + got[step, 1]
        return pair, pair + (got[step, 2] + got[step, 3])

    bulk, tail, whole = pl.ds(0, 640), pl.ds(640, 128), pl.ds(0, 768)
    half = pl.ds(0, 384)
    cuts = [0, near, (near + nleaf) // 2 + 2, nleaf]
    groups = len(cuts) - 1
    codes = []

    def code_round(step):
        copies = tree_copies(step, csend, crecv, code_ss, code_rs)
        for copy in copies:
            copy.start()
        return copies

    def code_levels(step, copies):
        for copy in copies:
            copy.wait()
        codes.extend(two_levels(csend[step], crecv, step))
        if step + 1 < rounds:
            csend[step + 1] = codes[-1]

    copies = code_round(0)
    exchange(send, recv, 0, 1, 0, near, bulk)
    pl.semaphore_wait(far_sem, 2)
    code_levels(0, copies)
    copies = code_round(1)

    for j in range(1, npanel):
        for copy in face_copies(j):
            copy.wait_recv()
    arriving = jnp.zeros((ROWS, 128), F32)
    for q in range(npanel - 1):
        slot = (me_p - q + npanel) % npanel
        tau = jnp.broadcast_to(tau_in[slot].reshape(56, 1, 128), (56, 2, 128)).reshape(ROWS, 128)
        swapped = pltpu.roll(tau, 64, 1)
        tau_re = jnp.where(low, tau, swapped)
        tau_im = jnp.where(low, -swapped, tau)
        value = arriving + face_in[slot].astype(F32)
        leaving = tau_re * value + tau_im * pltpu.roll(value, 64, 1)
        arriving = jnp.where(q < me_p, leaving, arriving)
    zero = jnp.zeros((ROWS, 128), F32)
    tile_re = src[:, 640:768].astype(F32) + jnp.where(low, zero, pltpu.roll(arriving, 64, 1))
    tile_im = src[:, 1408:1536].astype(F32) + jnp.where(low, zero, arriving)
    packed = dot(pick[0], tile_re.astype(BF16)) + dot(pick[1], tile_im.astype(BF16))
    send[:, :, 640:768] = packed.reshape(nleaf, 8, 128).astype(BF16)
    recv[0] = send[0]
    exchange(send, recv, 4, 1, 0, near, tail)
    exchange(send, recv, 1, 1, cuts[1], cuts[2], whole)
    code_levels(1, copies)
    if rounds > 2:
        copies = code_round(2)
    exchange(send, recv, 2, 1, cuts[2], cuts[3], whole)
    if rounds > 2:
        code_levels(2, copies)

    loads[1].wait()
    loads[2].wait()
    for level in range(levels):
        count = codes[level][0:1, 0:1]
        odd = (count - 2.0 * jnp.floor(count * 0.5)).astype(BF16)
        odd = jnp.broadcast_to(odd, (384, 384))
        for part in range(2):
            chosen[level, :, 384 * part : 384 * part + 384] = (
                sep[0, part] * (1 - odd) + sep[1, part] * odd
            )

    def combine(real, imag):
        real = real.reshape(-1, 8, 384)
        imag = pltpu.roll(imag.reshape(-1, 8, 384), 4, 1)
        return real + jnp.where(iota(imag.shape, 1) < 4, -1.0, 1.0) * imag

    by_row = jnp.zeros((NY, 8, 384), F32)
    for g in range(groups):
        first, last = cuts[g], cuts[g + 1]
        wait_for(a2a_rs, recv, g, first, last, bulk if g == 0 else whole)
        if g == 0:
            wait_for(a2a_rs, recv, 4 + g, first, last, tail)
        rows = recv[first:last].astype(F32).reshape((last - first) * 8, 768).astype(BF16)
        for part, back in ((0, back1), (1, back2)):
            cols = slice(part * 384, part * 384 + 384)
            result = combine(dot(rows, fac[0, :, cols]), dot(rows, fac[1, :, cols]))
            back[first:last] = result.astype(BF16)
            if part == 0:
                exchange(back1, ret1, 6 + g, -1, first, last, half)
                solved = back1[first:last].astype(F32).reshape(-1, NY, 8, 384)
                by_row = by_row + jnp.sum(solved, axis=0)
    ret1[0] = back1[0]
    ret2[0] = back2[0]
    eight = iota((8, 384), 0)

    def both_slots(rows):
        other = jnp.where(eight % 4 < 2, pltpu.roll(rows, 6, 0), pltpu.roll(rows, 2, 0))
        return rows + other

    for j in range(NY):
        ysend[j] = both_slots(by_row[j])
    row_copies = [
        pltpu.make_async_remote_copy(
            src_ref=ysend.at[j], dst_ref=erecv.at[3, j], send_sem=node_ss.at[3, j],
            recv_sem=node_rs.at[3, j], device_id=peer(j, -1), device_id_type=MESH,
        )
        for j in range(1, NY)
    ]
    for copy in row_copies:
        copy.start()
    for copy in row_copies:
        copy.wait()

    def node_round(step, value):
        esend[step] = value
        copies = tree_copies(step, esend, erecv, node_ss, node_rs)
        for copy in copies:
            copy.start()
        return copies

    turns = [1, 44, 64, 64]
    copies = node_round(0, ysend[0] + erecv[3, 1] + (erecv[3, 2] + erecv[3, 3]))
    exchange(back2, ret2, 10, -1, turns[0], turns[1], half)

    for g in range(groups):
        wait_for(a2a_rs, ret1, 6 + g, cuts[g], cuts[g + 1], half)
    vsend[0] = both_slots(jnp.sum(ret1[...].astype(F32), axis=0))
    trace_copies = tree_copies(0, vsend, vrecv, tree_ss, tree_rs)
    for copy in trace_copies:
        copy.start()
    for copy in copies:
        copy.wait()
    copies = node_round(1, two_levels(esend[0], erecv, 0)[1])
    exchange(back2, ret2, 10, -1, turns[1], turns[2], half)
    spots = iota((ROWS, nleaf * 8), 1)
    take = [(spots == spot + 4 * part).astype(F32).astype(BF16) for part in range(2)]
    rows = ret1[...].astype(F32).reshape(nleaf * 8, 384).astype(BF16)
    for part in range(2):
        top[part] = dot(take[part], rows)
    for copy in trace_copies:
        copy.wait()
    sums = list(two_levels(vsend[0], vrecv, 0))
    vsend[1] = sums[1]
    beside = tree_copies(1, vsend, vrecv, tree_ss, tree_rs)[0]
    beside.start()
    exchange(back2, ret2, 10, -1, turns[2], turns[3], half)
    for copy in copies:
        copy.wait()
    row_sum = two_levels(esend[1], erecv, 1)[1]
    copies = node_round(2, row_sum)
    exchange(back2, ret2, 10, -1, turns[3], nleaf, half)
    beside.wait()
    for copy in copies:
        copy.wait()
    sums += [vsend[1] + vrecv[1, 1], row_sum, *two_levels(row_sum, erecv, 2)]

    sign8 = jnp.where(eight < 4, -1.0, 1.0)
    value = jnp.zeros((8, 384), F32)
    for level in reversed(range(levels)):
        scale = 1.0 / math.sqrt(leaves * 2 ** (level + 1))
        operand = (sums[level] * scale - value).astype(BF16)
        both = dot(operand, chosen[level])
        value = both[:, 0:384] + sign8 * pltpu.roll(both[:, 384:768], 4, 0)

    even = iota((ROWS, 384), 0) % 2 == 0

    def store(quarter, values):
        values = values[0:used].reshape(leaves, 2, 384).astype(BF16)
        out_ref[0, :, :, 384 * quarter : 384 * quarter + 384] = values

    for part in range(2):
        shift = jnp.where(even, value[4 * part : 4 * part + 1], value[4 * part + 1 : 4 * part + 2])
        store(2 * part, top[part] - shift)
    wait_for(a2a_rs, ret2, 10, 0, nleaf, half)
    rows = ret2[...].astype(F32).reshape(nleaf * 8, 384).astype(BF16)
    for part in range(2):
        store(2 * part + 1, dot(take[part], rows))

    for g in range(groups):
        wait_for(a2a_ss, send, g, cuts[g], cuts[g + 1], bulk if g == 0 else whole)
        if g == 0:
            wait_for(a2a_ss, send, 4 + g, cuts[g], cuts[g + 1], tail)
        wait_for(a2a_ss, back1, 6 + g, cuts[g], cuts[g + 1], half)
    wait_for(a2a_ss, back2, 10, 0, nleaf, half)
    for j in range(1, npanel):
        for copy in face_copies(j):
            copy.wait_send()


def on_device(sources, transmission, media, sep_code, leaf_factors, sep_factors):
    leaves, shots, width2 = sources.shape[1:]
    npanel, nleaf = lax.axis_size("panel"), lax.axis_size("leaf")
    levels = nleaf.bit_length() - 1
    rounds = levels // 2
    half = width2 // 2
    sem = pltpu.SemaphoreType.DMA
    vmem = pl.BlockSpec(memory_space=pltpu.VMEM)
    hbm = pl.BlockSpec(memory_space=pl.ANY)
    return pl.pallas_call(
        functools.partial(kernel, (npanel, nleaf, levels, leaves)),
        out_shape=jax.ShapeDtypeStruct(sources.shape, BF16),
        in_specs=[hbm] * 6,
        out_specs=vmem,
        scratch_shapes=[
            pltpu.VMEM((leaves, 1, 128), F32),
            pltpu.VMEM((1, leaves), I32),
            pltpu.VMEM((1, 1), I32),
            pltpu.VMEM((leaves, shots, width2), BF16),
            pltpu.VMEM((ROWS, width2), BF16),
            pltpu.VMEM((2, half, half), BF16),
            pltpu.VMEM(sep_factors.shape, BF16),
            pltpu.VMEM((nleaf, 8, half), BF16),
            pltpu.VMEM((nleaf, 8, half), BF16),
            pltpu.VMEM((ROWS // 2, 128), F32),
            pltpu.VMEM((ROWS, 128), BF16),
            pltpu.VMEM((npanel, ROWS // 2, 128), F32),
            pltpu.VMEM((npanel, ROWS, 128), BF16),
            pltpu.VMEM((nleaf, 8, 384), BF16),
            pltpu.VMEM((nleaf, 8, 384), BF16),
            pltpu.VMEM((nleaf, 8, 384), BF16),
            pltpu.VMEM((nleaf, 8, 384), BF16),
            pltpu.VMEM((rounds, 8, 128), F32),
            pltpu.VMEM((rounds, 4, 8, 128), F32),
            pltpu.VMEM((rounds, 8, 384), F32),
            pltpu.VMEM((rounds, 4, 8, 384), F32),
            pltpu.VMEM((4, 8, 384), F32),
            pltpu.VMEM((3, 8, 384), F32),
            pltpu.VMEM((4, 4, 8, 384), F32),
            pltpu.VMEM((levels, 384, 768), BF16),
            pltpu.VMEM((2, ROWS, 384), F32),
            pltpu.SemaphoreType.REGULAR, sem((6,)), sem((npanel,)), sem((npanel,)), sem((npanel,)), sem((npanel,)),
            sem((11,)), sem((11,)), sem((rounds, 4)), sem((rounds, 4)), sem((rounds, 4)),
            sem((rounds, 4)), sem((4, 4)), sem((4, 4)),
        ],
        compiler_params=pltpu.CompilerParams(
            collective_id=0, has_side_effects=True, vmem_limit_bytes=67043328
        ),
    )(
        sources, transmission.transpose(1, 0, 2), media.reshape(1, leaves), sep_code,
        leaf_factors, sep_factors,
    )


def solution(mesh):
    return jax.shard_map(
        on_device,
        mesh=mesh,
        in_specs=(
            P("panel", "leaf", None, None),
            P("panel", "leaf", None),
            P("panel", "leaf", None),
            P("panel", "leaf"),
            P("leaf", None, None, None),
            P(),
        ),
        out_specs=P("panel", "leaf", None, None),
        check_vma=False,
    )
```

```python
import functools
import math

import jax
import jax.numpy as jnp
from jax import lax
from jax.experimental import pallas as pl
from jax.experimental.pallas import tpu as pltpu
from jax.sharding import PartitionSpec as P

NY = 4
ROWS = 112
MESH = pl.DeviceIdType.MESH
F32 = jnp.float32
BF16 = jnp.bfloat16
I32 = jnp.int32


def dot(a, b):
    return jnp.dot(a, b, preferred_element_type=F32)


def iota(shape, axis):
    return lax.broadcasted_iota(I32, shape, axis)


def kernel(
    sizes,
    src_hbm, tau_hbm, media_hbm, code_hbm, fac_hbm, sep_hbm,
    out_ref,
    tau_ref, media_ref, code_ref, raw, src, fac, sep, send, recv, tau_out, face_out, tau_in, face_in, back1, back2, ret1, ret2,
    csend, crecv, vsend, vrecv, ysend, esend, erecv, chosen, top,
    far_sem, load_sem, tau_ss, tau_rs, face_ss, face_rs, a2a_ss, a2a_rs, code_ss, code_rs, tree_ss, tree_rs,
    node_ss, node_rs,
):
    npanel, nleaf, levels, leaves = sizes
    nz = nleaf // NY
    used = 2 * leaves
    rounds = levels // 2
    me_p = lax.axis_index("panel")
    me = lax.axis_index("leaf")
    my_y, my_z = me // nz, me % nz

    def peer(k, sign):
        order = k // NY
        steps = (order % 2) * ((order + 1) // 2) - (1 - order % 2) * (order // 2)
        y = (my_y + sign * (k % NY) + NY) % NY
        z = (my_z + sign * steps + nz) % nz
        return {"panel": me_p, "leaf": y * nz + z}

    reach = nz // 4
    near = (2 * reach + 1) * NY

    def panel_peer(j):
        return {"panel": (me_p + j) % npanel, "leaf": me}

    barrier = pltpu.get_barrier_semaphore()

    @pl.loop(1, near)
    def _(k):
        pl.semaphore_signal(barrier, inc=1, device_id=peer(k, 1), device_id_type=MESH)

    for j in range(1, npanel):
        pl.semaphore_signal(barrier, inc=1, device_id=panel_peer(j), device_id_type=MESH)

    loads = [
        pltpu.make_async_copy(src_hbm.at[0], raw, load_sem.at[0]),
        pltpu.make_async_copy(fac_hbm.at[0], fac, load_sem.at[1]),
        pltpu.make_async_copy(sep_hbm, sep, load_sem.at[2]),
        pltpu.make_async_copy(media_hbm, media_ref, load_sem.at[3]),
        pltpu.make_async_copy(tau_hbm, tau_ref, load_sem.at[4]),
        pltpu.make_async_copy(code_hbm, code_ref, load_sem.at[5]),
    ]
    for load in loads:
        load.start()

    for load in loads[3:]:
        load.wait()
    lane = iota((ROWS, leaves), 1)
    leaf = iota((ROWS, leaves), 0) // 2
    kinds = jnp.broadcast_to(media_ref[...], (ROWS, leaves)).astype(F32)
    kind = jnp.sum(jnp.where(lane == leaf, kinds, 0.0), axis=1, keepdims=True)
    rank = jnp.sum(jnp.where((kinds == kind) & (lane < leaf), 1.0, 0.0), axis=1, keepdims=True)
    kind, rank = kind.astype(I32), rank.astype(I32)
    row = iota((ROWS, 1), 0)
    away_y = (kind // nz - my_y + NY) % NY
    away_z = (kind % nz - my_z + nz) % nz
    order = jnp.where(away_z <= nz // 2, 2 * away_z - 1, 2 * (nz - away_z))
    order = jnp.maximum(order, 0)
    spot = (order * NY + away_y) * 8 + rank * 2 + row % 2
    spot = jnp.where(row < used, spot, -64)
    diagonal = iota((ROWS, ROWS), 0) == iota((ROWS, ROWS), 1)
    spot_row = jnp.sum(jnp.where(diagonal, spot.astype(F32), 0.0), axis=0, keepdims=True).astype(I32)
    place = iota((nleaf * 8, ROWS), 0)
    pick = [(place == spot_row + 4 * part).astype(F32).astype(BF16) for part in range(2)]

    tau_out[0:leaves, :] = tau_ref[...].reshape(leaves, 128)
    tau_out[leaves:56, :] = jnp.zeros((56 - leaves, 128), F32)
    loads[0].wait()
    rows = raw[...].astype(F32).reshape(used, 1536)
    src[...] = jnp.concatenate([rows, jnp.zeros((ROWS - used, 1536), F32)], axis=0).astype(BF16)
    low = iota((ROWS, 128), 1) < 64
    tile_re, tile_im = src[:, 640:768].astype(F32), src[:, 1408:1536].astype(F32)
    face_out[...] = jnp.where(low, pltpu.roll(tile_re, 64, 1), tile_im).astype(BF16)
    packed = dot(pick[0], src[:, 0:640]) + dot(pick[1], src[:, 768:1408])
    send[:, :, 0:640] = packed.reshape(nleaf, 8, 640).astype(BF16)
    csend[0] = jnp.broadcast_to(code_ref[...].astype(F32), (8, 128))

    pl.semaphore_wait(barrier, near - 1 + npanel - 1)
    for order in (2 * reach - 1, 2 * reach):
        pl.semaphore_signal(far_sem, inc=1, device_id=peer(order * NY, 1), device_id_type=MESH)

    def face_copies(j):
        return [
            pltpu.make_async_remote_copy(
                src_ref=tau_out, dst_ref=tau_in.at[j], send_sem=tau_ss.at[j],
                recv_sem=tau_rs.at[j], device_id=panel_peer(j), device_id_type=MESH,
            ),
            pltpu.make_async_remote_copy(
                src_ref=face_out, dst_ref=face_in.at[j], send_sem=face_ss.at[j],
                recv_sem=face_rs.at[j], device_id=panel_peer(j), device_id_type=MESH,
            ),
        ]

    for j in range(1, npanel):
        for copy in face_copies(j):
            copy.start()

    def exchange(source, target, index, sign, first, last, cols):
        @pl.loop(max(first, 1), last)
        def _(k):
            pltpu.make_async_remote_copy(
                src_ref=source.at[k, :, cols], dst_ref=target.at[k, :, cols],
                send_sem=a2a_ss.at[index], recv_sem=a2a_rs.at[index],
                device_id=peer(k, sign), device_id_type=MESH,
            ).start()

    def wait_for(sems, buffer, index, first, last, cols):
        part = buffer.at[pl.ds(max(first, 1), last - max(first, 1)), :, cols]
        pltpu.make_async_copy(part, part, sems.at[index]).wait()

    def tree_copies(step, source, target, ss, rs):
        copies = []
        for j in range(1, 4):
            digit = me // 4**step % 4
            moved = (digit + 1 - 2 * (digit % 2), digit + 2 - 4 * (digit // 2), 3 - digit)[j - 1]
            other = me + (moved - digit) * 4**step
            copies.append(pltpu.make_async_remote_copy(
                src_ref=source.at[step], dst_ref=target.at[step, j], send_sem=ss.at[step, j],
                recv_sem=rs.at[step, j], device_id={"panel": me_p, "leaf": other},
                device_id_type=MESH,
            ))
        return copies

    def two_levels(own, got, step):
        pair = own + got[step, 1]
        return pair, pair + (got[step, 2] + got[step, 3])

    bulk, tail, whole = pl.ds(0, 640), pl.ds(640, 128), pl.ds(0, 768)
    half = pl.ds(0, 384)
    cuts = [0, near, (near + nleaf) // 2 + 2, nleaf]
    groups = len(cuts) - 1
    codes = []

    def code_round(step):
        copies = tree_copies(step, csend, crecv, code_ss, code_rs)
        for copy in copies:
            copy.start()
        return copies

    def code_levels(step, copies):
        for copy in copies:
            copy.wait()
        codes.extend(two_levels(csend[step], crecv, step))
        if step + 1 < rounds:
            csend[step + 1] = codes[-1]

    copies = code_round(0)
    exchange(send, recv, 0, 1, 0, near, bulk)
    pl.semaphore_wait(far_sem, 2)
    code_levels(0, copies)
    copies = code_round(1)

    for j in range(1, npanel):
        for copy in face_copies(j):
            copy.wait_recv()
    arriving = jnp.zeros((ROWS, 128), F32)
    for q in range(npanel - 1):
        slot = (me_p - q + npanel) % npanel
        tau = jnp.broadcast_to(tau_in[slot].reshape(56, 1, 128), (56, 2, 128)).reshape(ROWS, 128)
        swapped = pltpu.roll(tau, 64, 1)
        tau_re = jnp.where(low, tau, swapped)
        tau_im = jnp.where(low, -swapped, tau)
        value = arriving + face_in[slot].astype(F32)
        leaving = tau_re * value + tau_im * pltpu.roll(value, 64, 1)
        arriving = jnp.where(q < me_p, leaving, arriving)
    zero = jnp.zeros((ROWS, 128), F32)
    tile_re = src[:, 640:768].astype(F32) + jnp.where(low, zero, pltpu.roll(arriving, 64, 1))
    tile_im = src[:, 1408:1536].astype(F32) + jnp.where(low, zero, arriving)
    packed = dot(pick[0], tile_re.astype(BF16)) + dot(pick[1], tile_im.astype(BF16))
    send[:, :, 640:768] = packed.reshape(nleaf, 8, 128).astype(BF16)
    recv[0] = send[0]
    exchange(send, recv, 4, 1, 0, near, tail)
    exchange(send, recv, 1, 1, cuts[1], cuts[2], whole)
    code_levels(1, copies)
    if rounds > 2:
        copies = code_round(2)
    exchange(send, recv, 2, 1, cuts[2], cuts[3], whole)
    if rounds > 2:
        code_levels(2, copies)

    loads[1].wait()
    loads[2].wait()
    for level in range(levels):
        count = codes[level][0:1, 0:1]
        odd = (count - 2.0 * jnp.floor(count * 0.5)).astype(BF16)
        odd = jnp.broadcast_to(odd, (384, 384))
        for part in range(2):
            chosen[level, :, 384 * part : 384 * part + 384] = (
                sep[0, part] * (1 - odd) + sep[1, part] * odd
            )

    def combine(real, imag):
        real = real.reshape(-1, 8, 384)
        imag = pltpu.roll(imag.reshape(-1, 8, 384), 4, 1)
        return real + jnp.where(iota(imag.shape, 1) < 4, -1.0, 1.0) * imag

    by_row = jnp.zeros((NY, 8, 384), F32)
    for g in range(groups):
        first, last = cuts[g], cuts[g + 1]
        wait_for(a2a_rs, recv, g, first, last, bulk if g == 0 else whole)
        if g == 0:
            wait_for(a2a_rs, recv, 4 + g, first, last, tail)
        rows = recv[first:last].astype(F32).reshape((last - first) * 8, 768).astype(BF16)
        for part, back in ((0, back1), (1, back2)):
            cols = slice(part * 384, part * 384 + 384)
            result = combine(dot(rows, fac[0, :, cols]), dot(rows, fac[1, :, cols]))
            back[first:last] = result.astype(BF16)
            if part == 0:
                exchange(back1, ret1, 6 + g, -1, first, last, half)
                solved = back1[first:last].astype(F32).reshape(-1, NY, 8, 384)
                by_row = by_row + jnp.sum(solved, axis=0)
    ret1[0] = back1[0]
    ret2[0] = back2[0]
    eight = iota((8, 384), 0)

    def both_slots(rows):
        other = jnp.where(eight % 4 < 2, pltpu.roll(rows, 6, 0), pltpu.roll(rows, 2, 0))
        rows = rows + other
        return jnp.concatenate([rows[0:2], rows[4:6]], axis=0)

    for j in range(NY):
        ysend[j] = both_slots(by_row[j])
    row_copies = [
        pltpu.make_async_remote_copy(
            src_ref=ysend.at[j], dst_ref=erecv.at[3, j], send_sem=node_ss.at[3, j],
            recv_sem=node_rs.at[3, j], device_id=peer(j, -1), device_id_type=MESH,
        )
        for j in range(1, NY)
    ]
    for copy in row_copies:
        copy.start()
    for copy in row_copies:
        copy.wait()

    def node_round(step, value):
        esend[step] = value
        copies = tree_copies(step, esend, erecv, node_ss, node_rs)
        for copy in copies:
            copy.start()
        return copies

    turns = [1, 44, 64, 64]
    copies = node_round(0, ysend[0] + erecv[3, 1] + (erecv[3, 2] + erecv[3, 3]))
    exchange(back2, ret2, 10, -1, turns[0], turns[1], half)

    for g in range(groups):
        wait_for(a2a_rs, ret1, 6 + g, cuts[g], cuts[g + 1], half)
    vsend[0] = both_slots(jnp.sum(ret1[...].astype(F32), axis=0))
    trace_copies = tree_copies(0, vsend, vrecv, tree_ss, tree_rs)
    for copy in trace_copies:
        copy.start()
    for copy in copies:
        copy.wait()
    copies = node_round(1, two_levels(esend[0], erecv, 0)[1])
    exchange(back2, ret2, 10, -1, turns[1], turns[2], half)
    spots = iota((ROWS, nleaf * 8), 1)
    take = [(spots == spot + 4 * part).astype(F32).astype(BF16) for part in range(2)]
    rows = ret1[...].astype(F32).reshape(nleaf * 8, 384).astype(BF16)
    for part in range(2):
        top[part] = dot(take[part], rows)
    for copy in trace_copies:
        copy.wait()
    sums = list(two_levels(vsend[0], vrecv, 0))
    vsend[1] = sums[1]
    beside = tree_copies(1, vsend, vrecv, tree_ss, tree_rs)[0]
    beside.start()
    exchange(back2, ret2, 10, -1, turns[2], turns[3], half)
    for copy in copies:
        copy.wait()
    row_sum = two_levels(esend[1], erecv, 1)[1]
    copies = node_round(2, row_sum)
    exchange(back2, ret2, 10, -1, turns[3], nleaf, half)
    beside.wait()
    for copy in copies:
        copy.wait()
    sums += [vsend[1] + vrecv[1, 1], row_sum, *two_levels(row_sum, erecv, 2)]

    value = jnp.zeros((4, 384), F32)
    for level in reversed(range(levels)):
        scale = 1.0 / math.sqrt(leaves * 2 ** (level + 1))
        operand = (sums[level] * scale - value).astype(BF16)
        both = dot(operand, chosen[level])
        imag = both[:, 384:768]
        value = both[:, 0:384] + jnp.concatenate([-imag[2:4], imag[0:2]], axis=0)

    even = iota((ROWS, 384), 0) % 2 == 0

    def store(quarter, values):
        out_ref[:, 384 * quarter : 384 * quarter + 384] = values[0:used].astype(BF16)

    for part in range(2):
        shift = jnp.where(even, value[2 * part : 2 * part + 1], value[2 * part + 1 : 2 * part + 2])
        store(2 * part, top[part] - shift)
    wait_for(a2a_rs, ret2, 10, 0, nleaf, half)
    rows = ret2[...].astype(F32).reshape(nleaf * 8, 384).astype(BF16)
    for part in range(2):
        store(2 * part + 1, dot(take[part], rows))

    for g in range(groups):
        wait_for(a2a_ss, send, g, cuts[g], cuts[g + 1], bulk if g == 0 else whole)
        if g == 0:
            wait_for(a2a_ss, send, 4 + g, cuts[g], cuts[g + 1], tail)
        wait_for(a2a_ss, back1, 6 + g, cuts[g], cuts[g + 1], half)
    wait_for(a2a_ss, back2, 10, 0, nleaf, half)
    for j in range(1, npanel):
        for copy in face_copies(j):
            copy.wait_send()


def on_device(sources, transmission, media, sep_code, leaf_factors, sep_factors):
    leaves, shots, width2 = sources.shape[1:]
    npanel, nleaf = lax.axis_size("panel"), lax.axis_size("leaf")
    levels = nleaf.bit_length() - 1
    rounds = levels // 2
    half = width2 // 2
    sem = pltpu.SemaphoreType.DMA
    vmem = pl.BlockSpec(memory_space=pltpu.VMEM)
    hbm = pl.BlockSpec(memory_space=pl.ANY)
    out = pl.pallas_call(
        functools.partial(kernel, (npanel, nleaf, levels, leaves)),
        out_shape=jax.ShapeDtypeStruct((leaves * shots, width2), BF16),
        in_specs=[hbm] * 6,
        out_specs=vmem,
        scratch_shapes=[
            pltpu.VMEM((leaves, 1, 128), F32),
            pltpu.VMEM((1, leaves), I32),
            pltpu.VMEM((1, 1), I32),
            pltpu.VMEM((leaves, shots, width2), BF16),
            pltpu.VMEM((ROWS, width2), BF16),
            pltpu.VMEM((2, half, half), BF16),
            pltpu.VMEM(sep_factors.shape, BF16),
            pltpu.VMEM((nleaf, 8, half), BF16),
            pltpu.VMEM((nleaf, 8, half), BF16),
            pltpu.VMEM((ROWS // 2, 128), F32),
            pltpu.VMEM((ROWS, 128), BF16),
            pltpu.VMEM((npanel, ROWS // 2, 128), F32),
            pltpu.VMEM((npanel, ROWS, 128), BF16),
            pltpu.VMEM((nleaf, 8, 384), BF16),
            pltpu.VMEM((nleaf, 8, 384), BF16),
            pltpu.VMEM((nleaf, 8, 384), BF16),
            pltpu.VMEM((nleaf, 8, 384), BF16),
            pltpu.VMEM((rounds, 8, 128), F32),
            pltpu.VMEM((rounds, 4, 8, 128), F32),
            pltpu.VMEM((rounds, 4, 384), F32),
            pltpu.VMEM((rounds, 4, 4, 384), F32),
            pltpu.VMEM((4, 4, 384), F32),
            pltpu.VMEM((3, 4, 384), F32),
            pltpu.VMEM((4, 4, 4, 384), F32),
            pltpu.VMEM((levels, 384, 768), BF16),
            pltpu.VMEM((2, ROWS, 384), F32),
            pltpu.SemaphoreType.REGULAR, sem((6,)), sem((npanel,)), sem((npanel,)), sem((npanel,)), sem((npanel,)),
            sem((11,)), sem((11,)), sem((rounds, 4)), sem((rounds, 4)), sem((rounds, 4)),
            sem((rounds, 4)), sem((4, 4)), sem((4, 4)),
        ],
        compiler_params=pltpu.CompilerParams(
            collective_id=0, has_side_effects=True, vmem_limit_bytes=67043328
        ),
    )(
        sources, transmission.transpose(1, 0, 2), media.reshape(1, leaves), sep_code,
        leaf_factors, sep_factors,
    )
    return out.reshape(sources.shape)


def solution(mesh):
    return jax.shard_map(
        on_device,
        mesh=mesh,
        in_specs=(
            P("panel", "leaf", None, None),
            P("panel", "leaf", None),
            P("panel", "leaf", None),
            P("panel", "leaf"),
            P("leaf", None, None, None),
            P(),
        ),
        out_specs=P("panel", "leaf", None, None),
        check_vma=False,
    )
```
